32 devices in a mesh: pop: 8 (over z, x), grp: 4 (over y, core).
Axes of the slice: x: 2, y: 2, z: 4, core: 2. Of those that a mesh axis runs over, the one named last changes fastest.
Arguments:
- actions: bfloat16 [16384, 1024], P(('pop', 'grp')), may hold values from -6 to 6
- elite_mask: int32 [16384], P(('pop', 'grp')), may hold values from 0 to 1, as said below
- init_state: float32 [256], replicated, may hold values from -6 to 6
- w_state: bfloat16 [256, 256], replicated, may hold values from -0.375 to 0.375
- w_action: bfloat16 [32, 256], replicated, may hold values from -1 to 1
- bias: float32 [256], replicated, may hold values from -3 to 3
- w_out: bfloat16 [256, 256], replicated, may hold values from -0.375 to 0.375
- reward_vec: float32 [256], replicated, may hold values from -0.375 to 0.375
Outputs:
- new_mean: float32 [1024], replicated
- covariance: float32 [1024, 1024], P('pop')
- returns: float32 [16384], P(('pop', 'grp'))
The draws below stay inside these ranges and needn't reach their ends.
Inputs may be any that keep to these rules, and one draw needn't show every extreme that they name: `elite_mask`: each aligned block of 512 candidates (the candidates of one device) holds at least one elite.
All inputs are finite; a program needn't handle non-finite values.
Results may differ from the reference program's by a relative error of at most 0.0063.
Values sent between devices are 32-bit elements; how exact they have to be, the bound alone decides.
No kernel may reach another device: no remote copies, remote signals or barrier semaphores. Data moves between devices by JAX's collectives and lax.ppermute only.
A program may use at most 64 MiB of HBM per device.

```python
import jax
import jax.numpy as jnp
from jax import lax

ACT = 32
STEPS = 32
STATE = 256
HIDDEN_SIZE = 256
CAND_DEV = 512
DIM = 1024
POP = 16384


def draw_elite_mask(key, part):
    base = jax.random.randint(jax.random.fold_in(key, 11), (POP,), 0, 8)
    chosen = jax.random.randint(jax.random.fold_in(key, 12), (POP // CAND_DEV, 1), 0, CAND_DEV)
    position = jnp.arange(CAND_DEV, dtype=jnp.int32)[None, :]
    forced = (position == chosen).reshape(POP)
    return jnp.where(forced | (base == 0), 1, 0).astype(jnp.int32)


def raised(entries, rng, source, target, parts, factor):
    def block_of(axis_at):
        return (jnp.arange(entries.shape[axis_at]) // (entries.shape[axis_at] // parts)).reshape((-1,) + (1,) * (entries.ndim - 1 - axis_at))

    one_side = jax.random.permutation(rng, parts)[block_of(target)]
    second = (block_of(target) + parts // 2) % parts
    return jnp.where((block_of(source) == one_side) | (block_of(source) == second), factor * entries, entries)


def block_scale(key, extent, split, low, top_value):
    gain, own = 1.0, jax.random.fold_in(key, 6)
    for dim, parts in split:
        heights = jnp.exp(jax.random.uniform(jax.random.fold_in(own, dim), (parts,), jnp.float32, low / len(split), top_value / len(split)))
        gain = gain * jnp.repeat(heights, extent[dim] // parts).reshape([-1 if axis == dim else 1 for axis in range(len(extent))])
    return gain


def scatter_about(rng, dims, scale, limit, split=(), kind=jnp.bfloat16):
    drawn = jax.random.normal(rng, dims, jnp.float32) * scale
    if len(split) > 0:
        drawn = block_scale(rng, dims, split, -0.22, 0.18) * drawn
    return jnp.clip(drawn, min=-limit, max=limit).astype(kind)


def heavy_noise(stream_key, extent, width, most, pieces, heavy, held_as=jnp.bfloat16):
    entries = width * jax.random.normal(stream_key, extent, jnp.float32)
    if pieces:
        entries = entries * block_scale(stream_key, extent, pieces, -0.22, 0.18)
    return jnp.clip(raised(entries, jax.random.fold_in(stream_key, 3), *heavy), -most, most).astype(held_as)


def setup_inputs(seed: int = 0) -> dict:
    keys = jax.random.split(jax.random.key(seed), 9)
    return {
        "actions": heavy_noise(keys[0], (POP, DIM), 1.0, 6.0, ((0, 32),), (0, 1, 32, 2.75)),
        "elite_mask": draw_elite_mask(jax.random.fold_in(keys[8], 71), 0),
        "init_state": scatter_about(keys[2], (STATE,), 1.0, 6.0, (), jnp.float32),
        "w_state": scatter_about(keys[3], (STATE, HIDDEN_SIZE), STATE ** -0.5, 0.375),
        "w_action": scatter_about(keys[4], (ACT, HIDDEN_SIZE), ACT ** -0.5, 1.0),
        "bias": scatter_about(keys[5], (HIDDEN_SIZE,), 0.5, 3.0, (), jnp.float32),
        "w_out": scatter_about(keys[6], (HIDDEN_SIZE, STATE), HIDDEN_SIZE ** -0.5, 0.375),
        "reward_vec": scatter_about(keys[7], (STATE,), STATE ** -0.5, 0.375, (), jnp.float32),
    }


def reference(actions, elite_mask, init_state, w_state, w_action, bias, w_out, reward_vec):
    weight = elite_mask.astype(jnp.float32)
    weight_b = weight.astype(jnp.bfloat16)
    count = jnp.sum(weight)
    sums = jnp.dot(weight_b[None, :], actions, preferred_element_type=jnp.float32)[0]
    new_mean = sums / count
    masked = actions * weight_b[:, None]
    second = lax.dot_general(masked, actions, (((0,), (0,)), ((), ())), preferred_element_type=jnp.float32)
    covariance = second / count - new_mean[:, None] * new_mean[None, :]
    total_rows = actions.shape[0]
    per_step = jnp.transpose(actions.reshape(total_rows, STEPS, ACT), (1, 0, 2))
    start = jnp.broadcast_to(init_state[None, :], (total_rows, STATE)).astype(jnp.float32)

    def advance(carry, action_now):
        state, total = carry
        state_b = state.astype(jnp.bfloat16)
        pre = jnp.dot(state_b, w_state, preferred_element_type=jnp.float32)
        pre = pre + jnp.dot(action_now, w_action, preferred_element_type=jnp.float32) + bias
        hidden = jnp.tanh(pre).astype(jnp.bfloat16)
        state = 0.9 * state + jnp.dot(hidden, w_out, preferred_element_type=jnp.float32)
        total = total + jnp.sum(state * reward_vec[None, :], axis=1)
        return (state, total), None

    (final, total), unused = lax.scan(advance, (start, jnp.zeros((total_rows,), jnp.float32)), per_step)
    returns = total / STEPS
    return new_mean, covariance, returns
```

```python
import functools

import jax
import jax.numpy as jnp
from jax import lax
from jax.experimental import pallas as pl
from jax.experimental.pallas import tpu as pltpu
from jax.sharding import PartitionSpec as P

ALL = ("pop", "grp")
VMEM = pl.BlockSpec(memory_space=pltpu.VMEM)
SMEM = pl.BlockSpec(memory_space=pltpu.SMEM)


def bits_of(size):
    return [1 << k for k in range(size.bit_length() - 1)]


class Plan:
    def __init__(self, pops, grps, width):
        self.pops, self.grps, self.width = pops, grps, width
        self.side = grps // 2
        self.rows = width // pops
        self.cols = width // grps
        pop_dims = [("pop", m) for m in bits_of(pops)]
        grp_dims = [("grp", 2 * m) for m in bits_of(self.side)]
        dims = []
        for k in range(max(len(pop_dims), len(grp_dims))):
            dims += pop_dims[k : k + 1] + grp_dims[k : k + 1]
        other = list(dims)
        for k in range(0, len(dims) - 1, 2):
            other[k], other[k + 1] = dims[k + 1], dims[k]
        self.orders = (dims, other)
        self.phases = len(dims)
        self.blocks = 1 << self.phases
        self.masks = [[self.mask(order, p) for p in range(self.blocks)] for order in self.orders]
        last = max(k for order in self.orders for k, (axis, m) in enumerate(order) if axis == "grp") if grp_dims else -1
        self.run = 1 << (self.phases - 1 - last)

    def mask(self, order, p):
        pop = grp = 0
        for k, (axis, m) in enumerate(order):
            if p >> (len(order) - 1 - k) & 1:
                pop, grp = (pop ^ m, grp) if axis == "pop" else (pop, grp ^ m)
        return pop * self.side + grp // 2

    def pairs(self, of):
        out = []
        for p in range(self.pops):
            for g in range(self.grps):
                axis, m = of[g & 1]
                q, h = (p ^ m, g) if axis == "pop" else (p, g ^ m)
                out.append((p * self.grps + g, q * self.grps + h))
        return out


def moment_kernel(plan, base, count, with_sums, t_ref, w_ref, at_ref, a_ref, *refs):
    refs = list(refs)
    add_ref = None if with_sums is not None or len(refs) < 2 else refs.pop(0)
    out_ref = refs.pop(0)
    rows, cols, side = plan.rows, plan.cols, plan.side
    for first in range(0, count, plan.run):
        parts = []
        for k in range(plan.run):
            block = t_ref[base + first + k] // side
            parts.append(at_ref[pl.ds(pl.multiple_of(block * rows, rows), rows), :])
        lhs = jnp.concatenate(parts, axis=0) if len(parts) > 1 else parts[0]
        chunk = t_ref[plan.blocks] * side + lax.rem(t_ref[base + first], side)
        rhs = a_ref[:, pl.ds(pl.multiple_of(chunk * cols, cols), cols)]
        got = jnp.dot(lhs, rhs, preferred_element_type=jnp.float32)
        sl = pl.ds(first * rows, plan.run * rows)
        out_ref[sl, :] = got if add_ref is None else got + add_ref[sl, :]
    if with_sums is not None:
        sums_ref = refs.pop(0)
        w = w_ref[...].astype(jnp.float32)
        wide = jnp.broadcast_to(w, (16, w.shape[1])).astype(jnp.bfloat16)
        sums = jnp.dot(wide, a_ref[...], preferred_element_type=jnp.float32)
        for k in range(plan.width // 128):
            sums_ref[pl.ds(k, 1), :] = sums[0:1, k * 128 : (k + 1) * 128]
        total = jnp.sum(w, axis=1, keepdims=True)
        sums_ref[pl.ds(plan.width // 128, 8), :] = jnp.broadcast_to(total, (8, 128))


def moment(plan, table, weight, at, a, base, count, add=None, sums=False):
    shape = jax.ShapeDtypeStruct((count * plan.rows, plan.cols), jnp.float32)
    extra = jax.ShapeDtypeStruct((plan.width // 128 + 8, 128), jnp.float32)
    operands = [table, weight, at, a] + ([] if add is None else [add])
    flops = 2 * shape.shape[0] * shape.shape[1] * a.shape[0]
    return pl.pallas_call(
        functools.partial(moment_kernel, plan, base, count, True if sums else None),
        out_shape=(shape, extra) if sums else shape,
        in_specs=[SMEM] + [VMEM] * (len(operands) - 1),
        out_specs=(VMEM, VMEM) if sums else VMEM,
        compiler_params=pltpu.CompilerParams(vmem_limit_bytes=16 << 20),
        cost_estimate=pl.CostEstimate(flops=flops, bytes_accessed=4 << 20, transcendentals=0),
        name="moment",
    )(*operands)


def rollout_kernel(act, first, steps, scale, fresh, a_ref, ws_ref, wa_ref, b_ref, wo_ref, r_ref, *refs):
    per = 128 // act
    if fresh:
        s0_ref, out_refs = refs[0], refs[1:]
        rows = a_ref.shape[0]
        state = jnp.broadcast_to(s0_ref[...], (rows, s0_ref.shape[1]))
        total = jnp.zeros(state.shape, jnp.float32)
    else:
        out_refs = refs[2:]
        state, total = refs[0][...], refs[1][...]
    st_ref, sum_ref = out_refs[-2:]
    st_ref[...] = state
    sum_ref[...] = total

    def body(k, unused):
        off = pl.multiple_of(k * 128, 128)
        for j in range(per):
            st = st_ref[...]
            pre = jnp.dot(st.astype(jnp.bfloat16), ws_ref[...], preferred_element_type=jnp.float32)
            pre = pre + jnp.dot(a_ref[:, pl.ds(off, 128)], wa_ref[j], preferred_element_type=jnp.float32)
            hid = jnp.tanh(pre + b_ref[...]).astype(jnp.bfloat16)
            st = 0.9 * st + jnp.dot(hid, wo_ref[...], preferred_element_type=jnp.float32)
            st_ref[...] = st
            sum_ref[...] += st
        return unused

    lax.fori_loop(first // per, (first + steps) // per, body, 0)
    if scale is not None:
        out_refs[0][...] = jnp.sum(sum_ref[...] * r_ref[...], axis=1, keepdims=True) / scale


def rollout(carry, first, steps, scale, act, actions, init_state, w_state, wide_action, bias, w_out, reward_vec):
    rows, width = actions.shape[0], init_state.shape[1]
    hidden = w_out.shape[0]
    operands = [actions, w_state, wide_action, bias, w_out, reward_vec]
    operands += [init_state] if carry is None else list(carry)
    full = jax.ShapeDtypeStruct((rows, width), jnp.float32)
    last = scale is not None
    flops = 2 * rows * steps * (2 * width * hidden + 128 * hidden)
    return pl.pallas_call(
        functools.partial(rollout_kernel, act, first, steps, scale, carry is None),
        out_shape=jax.ShapeDtypeStruct((rows, 1), jnp.float32) if last else (full, full),
        in_specs=[VMEM] * len(operands),
        out_specs=VMEM if last else (VMEM, VMEM),
        scratch_shapes=[pltpu.VMEM((rows, width), jnp.float32)] * (2 if last else 0),
        compiler_params=pltpu.CompilerParams(vmem_limit_bytes=16 << 20),
        cost_estimate=pl.CostEstimate(flops=flops, bytes_accessed=3 << 20, transcendentals=rows * steps * hidden),
        name="rollout",
    )(*operands)


def finish_kernel(plan, t_ref, sums_ref, *refs):
    pieces, (mean_ref, cov_ref) = refs[:-2], refs[-2:]
    rows, cols, side, width = plan.rows, plan.cols, plan.side, plan.width
    lines = width // 128
    inv = sums_ref[pl.ds(lines, 1), :]
    mean = jnp.concatenate([sums_ref[pl.ds(k, 1), :] for k in range(lines)], axis=1) / jnp.concatenate([inv] * lines, axis=1)
    mean_ref[...] = mean
    pop, grp = t_ref[0], t_ref[1]
    line, inner = pop * rows // 128, lax.rem(pop * rows, 128)
    mine = sums_ref[pl.ds(line, 1), :] / inv
    column = jnp.transpose(jnp.broadcast_to(mine, (128, 128)))
    count = inv[:, 0:1]
    if rows < 128:
        choice = jnp.zeros((rows, 128), jnp.float32)
        for k in range(128 // rows):
            choice = jnp.where(inner == k * rows, column[k * rows : (k + 1) * rows], choice)
        column = choice
    for k, piece in enumerate(pieces):
        color, y = k // side, k % side
        at = (lax.rem(grp, 2) ^ color) * side + ((grp // 2) ^ y)
        start = pl.multiple_of(at * cols, cols)
        row = mean_ref[:, pl.ds(start, cols)]
        left = jnp.concatenate([column] * (cols // 128), axis=1)
        cov_ref[:, pl.ds(start, cols)] = piece[...] / count - left * row


def finish(plan, place, sums, pieces):
    return pl.pallas_call(
        functools.partial(finish_kernel, plan),
        out_shape=(jax.ShapeDtypeStruct((1, plan.width), jnp.float32), jax.ShapeDtypeStruct((plan.rows, plan.width), jnp.float32)),
        in_specs=[SMEM] + [VMEM] * (1 + len(pieces)),
        out_specs=(VMEM, VMEM),
        compiler_params=pltpu.CompilerParams(vmem_limit_bytes=8 << 20),
        name="finish",
    )(place, sums, *pieces)


def on_device(plan, actions, elite_mask, init_state, w_state, w_action, bias, w_out, reward_vec):
    act = w_action.shape[0]
    steps = actions.shape[1] // act
    pop, grp = lax.axis_index("pop"), lax.axis_index("grp")
    here = pop * plan.side + grp // 2
    color = grp % 2
    masks = jnp.array(plan.masks, jnp.int32)
    orders = here ^ masks

    def table(of):
        return jnp.concatenate([jnp.where(of == 0, orders[0], orders[1]), of[None]]).astype(jnp.int32)

    mine, theirs = table(color), table(1 - color)
    weight = elite_mask[None, :]
    at = jnp.transpose(actions * elite_mask.astype(jnp.bfloat16)[:, None])

    def send(x, of):
        return lax.ppermute(x, ALL, plan.pairs(of))

    core = (("grp", 1), ("grp", 1))
    half = plan.blocks // 2
    rows = plan.rows
    out_a, sums = moment(plan, theirs, weight, at, actions, half, half, sums=True)
    got_a = send(out_a, core)
    got_sums = send(sums, core)
    out_b = moment(plan, theirs, weight, at, actions, 0, half)
    got_b = send(out_b, core)
    ready = moment(plan, mine, weight, at, actions, half, half, add=got_a)
    kept = moment(plan, mine, weight, at, actions, 0, half)
    kept = kept + got_b
    sums = sums + got_sums

    per = 128 // act
    wide_action = jnp.stack([jnp.pad(w_action, ((j * act, 128 - (j + 1) * act), (0, 0))) for j in range(per)])
    fixed = (act, actions, init_state[None, :], w_state, wide_action, bias[None, :], w_out, reward_vec[None, :])
    cut = steps // 2
    carry = rollout(None, 0, cut, None, *fixed)
    returns = rollout(carry, cut, steps - cut, steps, *fixed)[:, 0]

    size = half
    chunks = [ready[half * rows // 2 :], ready[: half * rows // 2]]
    for k in range(plan.phases):
        of = (plan.orders[0][k], plan.orders[1][k])
        got = [send(c, of) for c in chunks]
        sums = sums + send(sums, of)
        if size == 1:
            mine_now = kept + got[0]
            break
        size //= 2
        upper = kept[size * rows :] + got[0]
        kept = kept[: size * rows] + got[1]
        if size > 1:
            chunks = [upper[size * rows // 2 :], upper[: size * rows // 2]]
        else:
            chunks = [upper]
    pieces = [mine_now]
    for m in bits_of(plan.side):
        pieces += [send(x, (("grp", 2 * m), ("grp", 2 * m))) for x in pieces]
    pieces += [send(x, core) for x in pieces]
    place = jnp.stack([pop, grp]).astype(jnp.int32)
    new_mean, covariance = finish(plan, place, sums, pieces)
    return (new_mean[0], covariance, returns)


def solution(mesh):
    placed = (P(ALL, None), P(ALL), P(), P(), P(), P(), P(), P())
    pops, grps = mesh.shape["pop"], mesh.shape["grp"]

    def run(actions, *rest):
        plan = Plan(pops, grps, actions.shape[1])
        return jax.shard_map(
            functools.partial(on_device, plan),
            mesh=mesh,
            in_specs=placed,
            out_specs=(P(), P("pop", None), P(ALL)),
            check_vma=False,
        )(actions, *rest)

    return run
```

```python
import functools

import jax
import jax.numpy as jnp
from jax import lax
from jax.experimental import pallas as pl
from jax.experimental.pallas import tpu as pltpu
from jax.sharding import PartitionSpec as P

ALL = ("pop", "grp")
CORE = (("grp", 1), ("grp", 1))
VMEM = pl.BlockSpec(memory_space=pltpu.VMEM)
SMEM = pl.BlockSpec(memory_space=pltpu.SMEM)
HBM = pl.BlockSpec(memory_space=pltpu.HBM)
PIECES = (4, 4, 4, 4, 4, 4, 4, 4)


def bits_of(size):
    return [1 << k for k in range(size.bit_length() - 1)]


class Plan:
    def __init__(self, pops, grps, width):
        self.pops, self.grps, self.width = pops, grps, width
        self.side = grps // 2
        self.rows = width // pops
        self.cols = width // grps
        pop_dims = [("pop", m) for m in bits_of(pops)]
        grp_dims = [("grp", 2 * m) for m in bits_of(self.side)]
        dims = []
        for k in range(max(len(pop_dims), len(grp_dims))):
            dims += pop_dims[k : k + 1] + grp_dims[k : k + 1]
        other = list(dims)
        for k in range(0, len(dims) - 1, 2):
            other[k], other[k + 1] = dims[k + 1], dims[k]
        self.orders = (dims, other)
        self.phases = len(dims)
        self.blocks = 1 << self.phases
        self.masks = [[self.mask(order, p) for p in range(self.blocks)] for order in self.orders]
        last = max([k for order in self.orders for k, (axis, m) in enumerate(order) if axis == "grp"], default=-1)
        self.run = 1 << (self.phases - 1 - last)
        self.chunks = []
        size = self.blocks
        while size > 1:
            size //= 2
            self.chunks.append([(size + size // 2, 2 * size), (size, size + size // 2)] if size > 1 else [(1, 2)])
        self.chunks.append([(0, 1)])

    def mask(self, order, p):
        pop = grp = 0
        for k, (axis, m) in enumerate(order):
            if p >> (len(order) - 1 - k) & 1:
                pop, grp = (pop ^ m, grp) if axis == "pop" else (pop, grp ^ m)
        return pop * self.side + grp // 2

    def pairs(self, of):
        out = []
        for p in range(self.pops):
            for g in range(self.grps):
                axis, m = of[g & 1]
                q, h = (p ^ m, g) if axis == "pop" else (p, g ^ m)
                out.append((p * self.grps + g, q * self.grps + h))
        return out


def moment_into(plan, place_ref, other, at_ref, a_ref, ranges, out_refs):
    rows, cols, side, run = plan.rows, plan.cols, plan.side, plan.run
    here = place_ref[0] * side + place_ref[1] // 2
    color = lax.rem(place_ref[1] + other, 2)
    where = {}
    for (lo, hi), ref in zip(ranges, out_refs, strict=True):
        for p in range(lo, hi):
            where[p] = (ref, (p - lo) * rows)
    for first in range(0, plan.blocks, run):
        if first not in where:
            continue
        places = [here ^ jnp.where(color == 0, plan.masks[0][first + k], plan.masks[1][first + k]) for k in range(run)]
        parts = [at_ref[pl.ds(pl.multiple_of(b // side * rows, rows), rows), :] for b in places]
        lhs = jnp.concatenate(parts, axis=0) if run > 1 else parts[0]
        chunk = color * side + lax.rem(places[0], side)
        rhs = a_ref[:, pl.ds(pl.multiple_of(chunk * cols, cols), cols)]
        got = jnp.dot(lhs, rhs, preferred_element_type=jnp.float32)
        for k in range(run):
            ref, at = where[first + k]
            ref[pl.ds(at, rows), :] = got[k * rows : (k + 1) * rows]


def first_kernel(plan, ranges, cuts, place_ref, w_hbm, a_hbm, a_ref, at_ref, sums_ref, *refs):
    out_refs, (w_ref, sems) = refs[:-2], refs[-2:]
    height = a_ref.shape[0] // cuts
    copies = [pltpu.make_async_copy(w_hbm, w_ref, sems.at[cuts])]
    for k in range(cuts):
        sl = pl.ds(k * height, height)
        copies.append(pltpu.make_async_copy(a_hbm.at[sl, :], a_ref.at[sl, :], sems.at[k]))
    for copy in copies:
        copy.start()
    copies[0].wait()
    w = w_ref[...].astype(jnp.float32)
    wide = w.astype(jnp.bfloat16)
    for k in range(cuts):
        copies[k + 1].wait()
        sl = pl.ds(k * height, height)
        for c in range(plan.width // 128):
            turned = jnp.transpose(a_ref[sl, c * 128 : (c + 1) * 128])
            at_ref[pl.ds(c * 128, 128), sl] = turned * wide[:, k * height : (k + 1) * height]
    moment_into(plan, place_ref, 1, at_ref, a_ref, ranges, out_refs)
    tall = jnp.broadcast_to(w, (16, w.shape[1])).astype(jnp.bfloat16)
    sums = jnp.dot(tall, a_ref[...], preferred_element_type=jnp.float32)
    lines = plan.width // 128
    for k in range(lines):
        sums_ref[pl.ds(k, 1), :] = sums[0:1, k * 128 : (k + 1) * 128]
    total = jnp.sum(w, axis=1, keepdims=True)
    sums_ref[pl.ds(lines, 8), :] = jnp.broadcast_to(total, (8, 128))


def f32(*shape):
    return jax.ShapeDtypeStruct(shape, jnp.float32)


def first(plan, place, weight, actions, ranges):
    count, width = actions.shape
    cuts = max(1, min(4, count // 128))
    held = jax.ShapeDtypeStruct((count, width), jnp.bfloat16)
    turned = jax.ShapeDtypeStruct((width, count), jnp.bfloat16)
    outs = [held, turned, f32(width // 128 + 8, 128)] + [f32((hi - lo) * plan.rows, plan.cols) for lo, hi in ranges]
    return pl.pallas_call(
        functools.partial(first_kernel, plan, ranges, cuts),
        out_shape=outs,
        in_specs=[SMEM, HBM, HBM],
        out_specs=[VMEM] * len(outs),
        scratch_shapes=[pltpu.VMEM((1, count), jnp.int32), pltpu.SemaphoreType.DMA((cuts + 1,))],
        compiler_params=pltpu.CompilerParams(vmem_limit_bytes=16 << 20),
        cost_estimate=pl.CostEstimate(flops=1 << 29, bytes_accessed=4 << 20, transcendentals=0),
        name="first",
    )(place, pltpu.with_memory_space_constraint(weight, pltpu.HBM), pltpu.with_memory_space_constraint(actions, pltpu.HBM))


def second_kernel(plan, theirs, ours, place_ref, at_ref, a_ref, *refs):
    moment_into(plan, place_ref, 1, at_ref, a_ref, theirs, refs[: len(theirs)])
    moment_into(plan, place_ref, 0, at_ref, a_ref, ours, refs[len(theirs) :])


def second(plan, place, at, actions, theirs, ours):
    outs = [f32((hi - lo) * plan.rows, plan.cols) for lo, hi in theirs + ours]
    got = pl.pallas_call(
        functools.partial(second_kernel, plan, theirs, ours),
        out_shape=outs,
        in_specs=[SMEM, VMEM, VMEM],
        out_specs=[VMEM] * len(outs),
        compiler_params=pltpu.CompilerParams(vmem_limit_bytes=16 << 20),
        cost_estimate=pl.CostEstimate(flops=3 << 29, bytes_accessed=6 << 20, transcendentals=0),
        name="second",
    )(place, at, actions)
    return got[: len(theirs)], got[len(theirs) :]


def rollout_kernel(act, first, steps, scale, fresh, a_ref, ws_ref, wa_ref, b_ref, wo_ref, r_ref, *refs):
    per = 128 // act
    if fresh:
        s0_ref, out_refs = refs[0], refs[1:]
        rows = a_ref.shape[0]
        state = jnp.broadcast_to(s0_ref[...], (rows, s0_ref.shape[1]))
        total = jnp.zeros(state.shape, jnp.float32)
    else:
        out_refs = refs[2:]
        state, total = refs[0][...], refs[1][...]
    st_ref, sum_ref = out_refs[-2:]
    st_ref[...] = state
    sum_ref[...] = total

    def body(k, unused):
        off = pl.multiple_of(k * 128, 128)
        for j in range(per):
            st = st_ref[...]
            pre = jnp.dot(st.astype(jnp.bfloat16), ws_ref[...], preferred_element_type=jnp.float32)
            pre = pre + jnp.dot(a_ref[:, pl.ds(off, 128)], wa_ref[j], preferred_element_type=jnp.float32)
            hid = jnp.tanh(pre + b_ref[...]).astype(jnp.bfloat16)
            st = 0.9 * st + jnp.dot(hid, wo_ref[...], preferred_element_type=jnp.float32)
            st_ref[...] = st
            sum_ref[...] += st
        return unused

    lax.fori_loop(first // per, (first + steps) // per, body, 0)
    if scale is not None:
        weighted = sum_ref[...] * r_ref[...]
        ones = jnp.ones((8, weighted.shape[1]), jnp.float32)
        line = lax.dot_general(ones, weighted, (((1,), (1,)), ((), ())), precision=lax.Precision.HIGHEST)
        out_refs[0][...] = line[0:1] / scale


def rollout(carry, first, steps, scale, act, actions, init_state, w_state, wide_action, bias, w_out, reward_vec):
    rows, width = actions.shape[0], init_state.shape[1]
    hidden = w_out.shape[0]
    operands = [actions, w_state, wide_action, bias, w_out, reward_vec]
    operands += [init_state] if carry is None else list(carry)
    last = scale is not None
    flops = 2 * rows * steps * (2 * width * hidden + 128 * hidden)
    return pl.pallas_call(
        functools.partial(rollout_kernel, act, first, steps, scale, carry is None),
        out_shape=f32(1, rows) if last else (f32(rows, width), f32(rows, width)),
        in_specs=[VMEM] * len(operands),
        out_specs=VMEM if last else (VMEM, VMEM),
        scratch_shapes=[pltpu.VMEM((rows, width), jnp.float32)] * (2 if last else 0),
        compiler_params=pltpu.CompilerParams(vmem_limit_bytes=16 << 20),
        cost_estimate=pl.CostEstimate(flops=flops, bytes_accessed=1 << 20, transcendentals=rows * steps * hidden),
        name="rollout",
    )(*operands)


def finish_kernel(plan, place_ref, sums_ref, *refs):
    pieces, (mean_ref, cov_ref) = refs[:-2], refs[-2:]
    rows, cols, side, width = plan.rows, plan.cols, plan.side, plan.width
    lines = width // 128
    count = sums_ref[pl.ds(lines, 1), :]
    inverse = 1.0 / count[:, 0:1]
    means = sums_ref[pl.ds(0, lines), :] / count
    mean_ref[...] = jnp.concatenate([means[k : k + 1] for k in range(lines)], axis=1)
    pop, grp = place_ref[0], place_ref[1]
    line, inner = pop * rows // 128, lax.rem(pop * rows, 128)
    mine = sums_ref[pl.ds(line, 1), :] / count
    column = jnp.transpose(jnp.broadcast_to(mine, (128, 128)))
    if rows < 128:
        choice = jnp.zeros((rows, 128), jnp.float32)
        for k in range(128 // rows):
            choice = jnp.where(inner == k * rows, column[k * rows : (k + 1) * rows], choice)
        column = choice
    left = jnp.concatenate([column] * (cols // 128), axis=1)
    for k, piece in enumerate(pieces):
        color, y = k // side, k % side
        at = (lax.rem(grp, 2) ^ color) * side + ((grp // 2) ^ y)
        sl = pl.ds(pl.multiple_of(at * cols, cols), cols)
        cov_ref[:, sl] = piece[...] * inverse - left * mean_ref[:, sl]


def finish(plan, place, sums, pieces):
    return pl.pallas_call(
        functools.partial(finish_kernel, plan),
        out_shape=(f32(1, plan.width), f32(plan.rows, plan.width)),
        in_specs=[SMEM] + [VMEM] * (1 + len(pieces)),
        out_specs=(VMEM, VMEM),
        compiler_params=pltpu.CompilerParams(vmem_limit_bytes=8 << 20),
        name="finish",
    )(place, sums, *pieces)


def on_device(plan, actions, elite_mask, init_state, w_state, w_action, bias, w_out, reward_vec):
    act = w_action.shape[0]
    steps = actions.shape[1] // act
    rows, phases, chunks = plan.rows, plan.phases, plan.chunks
    place = jnp.stack([lax.axis_index("pop"), lax.axis_index("grp")]).astype(jnp.int32)

    def send(x, of):
        return lax.ppermute(x, ALL, plan.pairs(of))

    rest = [(0, plan.blocks // 2)]
    ours = [r for level in chunks for r in level]
    actions, at, sums, *outs = first(plan, place, elite_mask[None, :], actions, chunks[0])
    got = [(r, send(x, CORE)) for r, x in zip(chunks[0], outs, strict=True)]
    sums = sums + send(sums, CORE)
    theirs, own = second(plan, place, at, actions, rest, ours)
    got.append((rest[0], send(theirs[0], CORE)))
    own = dict(zip(ours, own, strict=True))

    def total(lo, hi):
        out = own[lo, hi]
        for (a, b), x in got:
            if a <= lo and hi <= b:
                out = out + x[(lo - a) * rows : (hi - a) * rows]
        return out

    per = 128 // act
    wide_action = jnp.stack([jnp.pad(w_action, ((j * act, 128 - (j + 1) * act), (0, 0))) for j in range(per)])
    fixed = (act, actions, init_state[None, :], w_state, wide_action, bias[None, :], w_out, reward_vec[None, :])
    done, carry = 0, None
    for i, piece in enumerate(PIECES):
        last = i == len(PIECES) - 1
        piece = steps - done if last else piece * steps // sum(PIECES) // per * per
        carry = rollout(carry, done, piece, steps if last else None, *fixed)
        done += piece
    returns = carry[0]

    for k in range(phases):
        of = (plan.orders[0][k], plan.orders[1][k])
        sums = sums + send(sums, of)
        for lo, hi in chunks[k]:
            x = total(lo, hi)
            base = 0 if hi - lo == 1 << (phases - 1 - k) else lo - (1 << (phases - 1 - k))
            got.append(((base, base + hi - lo), send(x, of)))
    pieces = [total(0, 1)]
    for m in bits_of(plan.side):
        pieces += [send(x, (("grp", 2 * m), ("grp", 2 * m))) for x in pieces]
    pieces += [send(x, CORE) for x in pieces]
    new_mean, covariance = finish(plan, place, sums, pieces)
    return (new_mean[0], covariance, returns)


def solution(mesh):
    placed = (P(ALL, None), P(ALL), P(), P(), P(), P(), P(), P())
    pops, grps = mesh.shape["pop"], mesh.shape["grp"]

    def run(actions, *rest):
        plan = Plan(pops, grps, actions.shape[1])

        def body(*args):
            return on_device(plan, *args)

        return jax.shard_map(
            body, mesh=mesh, in_specs=placed, out_specs=(P(), P("pop", None), P(ALL)), check_vma=False
        )(actions, *rest)

    return run
```

```python
import functools

import jax
import jax.numpy as jnp
from jax import lax
from jax.experimental import pallas as pl
from jax.experimental.pallas import tpu as pltpu
from jax.sharding import PartitionSpec as P

ALL = ("pop", "grp")
CORE = (("grp", 1), ("grp", 1))
VMEM = pl.BlockSpec(memory_space=pltpu.VMEM)
SMEM = pl.BlockSpec(memory_space=pltpu.SMEM)
HBM = pl.BlockSpec(memory_space=pltpu.HBM)
PIECES = (4, 4, 4, 4, 4, 4, 4, 4)


def bits_of(size):
    return [1 << k for k in range(size.bit_length() - 1)]


class Plan:
    def __init__(self, pops, grps, width):
        self.pops, self.grps, self.width = pops, grps, width
        self.side = grps // 2
        self.rows = width // pops
        self.cols = width // grps
        self.tail = (width // self.cols + 1 + 7) // 8 * 8
        pop_dims = [("pop", m) for m in bits_of(pops)]
        grp_dims = [("grp", 2 * m) for m in bits_of(self.side)]
        dims = []
        for k in range(max(len(pop_dims), len(grp_dims))):
            dims += pop_dims[k : k + 1] + grp_dims[k : k + 1]
        other = list(dims)
        for k in range(0, len(dims) - 1, 2):
            other[k], other[k + 1] = dims[k + 1], dims[k]
        self.orders = (dims, other)
        self.phases = len(dims)
        self.blocks = 1 << self.phases
        self.masks = [[self.mask(order, p) for p in range(self.blocks)] for order in self.orders]
        last = max([k for order in self.orders for k, (axis, m) in enumerate(order) if axis == "grp"], default=-1)
        self.run = 1 << (self.phases - 1 - last)
        self.chunks = []
        size = self.blocks
        while size > 1:
            size //= 2
            self.chunks.append([(size + size // 2, 2 * size), (size, size + size // 2)] if size > 1 else [(1, 2)])
        self.chunks.append([(0, 1)])

    def mask(self, order, p):
        pop = grp = 0
        for k, (axis, m) in enumerate(order):
            if p >> (len(order) - 1 - k) & 1:
                pop, grp = (pop ^ m, grp) if axis == "pop" else (pop, grp ^ m)
        return pop * self.side + grp // 2

    def pairs(self, of):
        out = []
        for p in range(self.pops):
            for g in range(self.grps):
                axis, m = of[g & 1]
                q, h = (p ^ m, g) if axis == "pop" else (p, g ^ m)
                out.append((p * self.grps + g, q * self.grps + h))
        return out


def moment_into(plan, place_ref, other, at_ref, a_ref, ranges, out_refs):
    rows, cols, side, run = plan.rows, plan.cols, plan.side, plan.run
    here = place_ref[0] * side + place_ref[1] // 2
    color = lax.rem(place_ref[1] + other, 2)
    where = {}
    for (lo, hi), ref in zip(ranges, out_refs, strict=True):
        for p in range(lo, hi):
            where[p] = (ref, (p - lo) * rows)
    for first in range(0, plan.blocks, run):
        if first not in where:
            continue
        places = [here ^ jnp.where(color == 0, plan.masks[0][first + k], plan.masks[1][first + k]) for k in range(run)]
        parts = [at_ref[pl.ds(pl.multiple_of(b // side * rows, rows), rows), :] for b in places]
        lhs = jnp.concatenate(parts, axis=0) if run > 1 else parts[0]
        chunk = color * side + lax.rem(places[0], side)
        rhs = a_ref[:, pl.ds(pl.multiple_of(chunk * cols, cols), cols)]
        got = jnp.dot(lhs, rhs, preferred_element_type=jnp.float32)
        for k in range(run):
            ref, at = where[first + k]
            ref[pl.ds(at, rows), :] = got[k * rows : (k + 1) * rows]


def first_kernel(plan, ranges, cuts, place_ref, w_hbm, a_hbm, a_ref, at_ref, *refs):
    out_refs, (w_ref, sems) = refs[:-2], refs[-2:]
    height = a_ref.shape[0] // cuts
    copies = [pltpu.make_async_copy(w_hbm, w_ref, sems.at[cuts])]
    for k in range(cuts):
        sl = pl.ds(k * height, height)
        copies.append(pltpu.make_async_copy(a_hbm.at[sl, :], a_ref.at[sl, :], sems.at[k]))
    for copy in copies:
        copy.start()
    copies[0].wait()
    w = w_ref[...].astype(jnp.float32)
    wide = w.astype(jnp.bfloat16)
    for k in range(cuts):
        copies[k + 1].wait()
        sl = pl.ds(k * height, height)
        for c in range(plan.width // 128):
            turned = jnp.transpose(a_ref[sl, c * 128 : (c + 1) * 128])
            at_ref[pl.ds(c * 128, 128), sl] = turned * wide[:, k * height : (k + 1) * height]
    moment_into(plan, place_ref, 1, at_ref, a_ref, ranges, out_refs)
    tall = jnp.broadcast_to(w, (16, w.shape[1])).astype(jnp.bfloat16)
    sums = jnp.dot(tall, a_ref[...], preferred_element_type=jnp.float32)
    lo, hi = ranges[0]
    base, cols = (hi - lo) * plan.rows, plan.cols
    for k in range(plan.width // cols):
        out_refs[0][pl.ds(base + k, 1), :] = sums[0:1, k * cols : (k + 1) * cols]
    left = plan.tail - plan.width // cols
    total = jnp.sum(w, axis=1, keepdims=True)
    out_refs[0][pl.ds(base + plan.width // cols, left), :] = jnp.broadcast_to(total, (left, cols))


def f32(*shape):
    return jax.ShapeDtypeStruct(shape, jnp.float32)


def first(plan, place, weight, actions, ranges):
    count, width = actions.shape
    cuts = max(1, min(4, count // 128))
    held = jax.ShapeDtypeStruct((count, width), jnp.bfloat16)
    turned = jax.ShapeDtypeStruct((width, count), jnp.bfloat16)
    outs = [held, turned]
    outs += [f32((hi - lo) * plan.rows + (0 if i else plan.tail), plan.cols) for i, (lo, hi) in enumerate(ranges)]
    return pl.pallas_call(
        functools.partial(first_kernel, plan, ranges, cuts),
        out_shape=outs,
        in_specs=[SMEM, HBM, HBM],
        out_specs=[VMEM] * len(outs),
        scratch_shapes=[pltpu.VMEM((1, count), jnp.int32), pltpu.SemaphoreType.DMA((cuts + 1,))],
        compiler_params=pltpu.CompilerParams(vmem_limit_bytes=16 << 20),
        cost_estimate=pl.CostEstimate(flops=1 << 29, bytes_accessed=4 << 20, transcendentals=0),
        name="first",
    )(place, pltpu.with_memory_space_constraint(weight, pltpu.HBM), pltpu.with_memory_space_constraint(actions, pltpu.HBM))


def later_kernel(plan, theirs, ours, place_ref, at_ref, a_ref, *refs):
    moment_into(plan, place_ref, 1, at_ref, a_ref, theirs, refs[: len(theirs)])
    moment_into(plan, place_ref, 0, at_ref, a_ref, ours, refs[len(theirs) :])


def later(plan, place, at, actions, theirs, ours):
    outs = [f32((hi - lo) * plan.rows, plan.cols) for lo, hi in theirs + ours]
    got = pl.pallas_call(
        functools.partial(later_kernel, plan, theirs, ours),
        out_shape=outs,
        in_specs=[SMEM, VMEM, VMEM],
        out_specs=[VMEM] * len(outs),
        compiler_params=pltpu.CompilerParams(vmem_limit_bytes=16 << 20),
        cost_estimate=pl.CostEstimate(flops=1 << 29, bytes_accessed=4 << 20, transcendentals=0),
        name="later",
    )(place, at, actions)
    return got[: len(theirs)], got[len(theirs) :]


def combine_kernel(size, tail, offsets, ends, *refs):
    own_ref, out_ref = refs[0], refs[-1]
    terms, (mine_ref, got_ref) = refs[1:-3], refs[-3:-1]
    out = own_ref[...]
    for ref, at in zip(terms, offsets, strict=True):
        out = out + ref[pl.ds(at, size), :]
    out_ref[pl.ds(0, size), :] = out
    out_ref[pl.ds(size, tail), :] = mine_ref[pl.ds(ends[0], tail), :] + got_ref[pl.ds(ends[1], tail), :]


def combine(plan, own, terms, mine, got):
    size = own.shape[0]
    ends = (mine.shape[0] - plan.tail, got.shape[0] - plan.tail)
    operands = [own] + [x for x, _ in terms] + [mine, got]
    return pl.pallas_call(
        functools.partial(combine_kernel, size, plan.tail, [at for _, at in terms], ends),
        out_shape=f32(size + plan.tail, plan.cols),
        in_specs=[VMEM] * len(operands),
        out_specs=VMEM,
        compiler_params=pltpu.CompilerParams(vmem_limit_bytes=8 << 20),
        cost_estimate=pl.CostEstimate(flops=1 << 18, bytes_accessed=1 << 18, transcendentals=0),
        name="combine",
    )(*operands)


def rollout_kernel(act, first, steps, scale, fresh, a_ref, ws_ref, wa_ref, b_ref, wo_ref, r_ref, *refs):
    per = 128 // act
    if fresh:
        s0_ref, out_refs = refs[0], refs[1:]
        rows = a_ref.shape[0]
        state = jnp.broadcast_to(s0_ref[...], (rows, s0_ref.shape[1]))
        total = jnp.zeros(state.shape, jnp.float32)
    else:
        out_refs = refs[2:]
        state, total = refs[0][...], refs[1][...]
    st_ref, sum_ref = out_refs[-2:]
    st_ref[...] = state
    sum_ref[...] = total

    def body(k, unused):
        off = pl.multiple_of(k * 128, 128)
        for j in range(per):
            st = st_ref[...]
            pre = jnp.dot(st.astype(jnp.bfloat16), ws_ref[...], preferred_element_type=jnp.float32)
            pre = pre + jnp.dot(a_ref[:, pl.ds(off, 128)], wa_ref[j], preferred_element_type=jnp.float32)
            hid = jnp.tanh(pre + b_ref[...]).astype(jnp.bfloat16)
            st = 0.9 * st + jnp.dot(hid, wo_ref[...], preferred_element_type=jnp.float32)
            st_ref[...] = st
            sum_ref[...] += st
        return unused

    lax.fori_loop(first // per, (first + steps) // per, body, 0)
    if scale is not None:
        weighted = sum_ref[...] * r_ref[...]
        ones = jnp.ones((8, weighted.shape[1]), jnp.float32)
        line = lax.dot_general(ones, weighted, (((1,), (1,)), ((), ())), precision=lax.Precision.HIGHEST)
        out_refs[0][...] = line[0:1] / scale


def rollout(carry, first, steps, scale, act, actions, init_state, w_state, wide_action, bias, w_out, reward_vec):
    rows, width = actions.shape[0], init_state.shape[1]
    hidden = w_out.shape[0]
    operands = [actions, w_state, wide_action, bias, w_out, reward_vec]
    operands += [init_state] if carry is None else list(carry)
    last = scale is not None
    flops = 2 * rows * steps * (2 * width * hidden + 128 * hidden)
    return pl.pallas_call(
        functools.partial(rollout_kernel, act, first, steps, scale, carry is None),
        out_shape=f32(1, rows) if last else (f32(rows, width), f32(rows, width)),
        in_specs=[VMEM] * len(operands),
        out_specs=VMEM if last else (VMEM, VMEM),
        scratch_shapes=[pltpu.VMEM((rows, width), jnp.float32)] * (2 if last else 0),
        compiler_params=pltpu.CompilerParams(vmem_limit_bytes=16 << 20),
        cost_estimate=pl.CostEstimate(flops=flops, bytes_accessed=1 << 20, transcendentals=rows * steps * hidden),
        name="rollout",
    )(*operands)


def finish_kernel(plan, ends, place_ref, mine_ref, got_ref, *refs):
    pieces, (mean_ref, cov_ref, line_ref) = refs[:-3], refs[-3:]
    rows, cols, side = plan.rows, plan.cols, plan.side
    tail = mine_ref[pl.ds(ends[0], plan.tail), :] + got_ref[pl.ds(ends[1], plan.tail), :]
    lines = plan.width // cols
    count = tail[lines : lines + 1]
    inverse = 1.0 / count[:, 0:1]
    for k in range(lines):
        mean_ref[:, pl.ds(k * cols, cols)] = tail[k : k + 1] / count
    pop, grp = place_ref[0], place_ref[1]
    start = pl.multiple_of(pop * rows // 128 * 128, 128)
    column = jnp.transpose(jnp.broadcast_to(mean_ref[:, pl.ds(start, 128)], (128, 128)))
    if rows < 128:
        line_ref[...] = column
        column = line_ref[pl.ds(pl.multiple_of(lax.rem(pop * rows, 128), rows), rows), :]
    left = jnp.concatenate([column] * (cols // 128), axis=1)
    for k, piece in enumerate(pieces):
        color, y = k // side, k % side
        at = (lax.rem(grp, 2) ^ color) * side + ((grp // 2) ^ y)
        sl = pl.ds(pl.multiple_of(at * cols, cols), cols)
        cov_ref[:, sl] = piece[...] * inverse - left * mean_ref[:, sl]


def finish(plan, place, mine, got, pieces):
    ends = (mine.shape[0] - plan.tail, got.shape[0] - plan.tail)
    return pl.pallas_call(
        functools.partial(finish_kernel, plan, ends),
        out_shape=(f32(1, plan.width), f32(plan.rows, plan.width)),
        in_specs=[SMEM] + [VMEM] * (2 + len(pieces)),
        out_specs=(VMEM, VMEM),
        scratch_shapes=[pltpu.VMEM((128, 128), jnp.float32)],
        compiler_params=pltpu.CompilerParams(vmem_limit_bytes=8 << 20),
        name="finish",
    )(place, mine, got, *pieces)


def on_device(plan, actions, elite_mask, init_state, w_state, w_action, bias, w_out, reward_vec):
    act = w_action.shape[0]
    steps = actions.shape[1] // act
    rows, phases, chunks = plan.rows, plan.phases, plan.chunks
    place = jnp.stack([lax.axis_index("pop"), lax.axis_index("grp")]).astype(jnp.int32)

    def send(x, of):
        return lax.ppermute(x, ALL, plan.pairs(of))

    rest = [(0, plan.blocks // 2)]
    actions, at, *outs = first(plan, place, elite_mask[None, :], actions, chunks[0])
    got = [(r, send(x, CORE)) for r, x in zip(chunks[0], outs, strict=True)]
    payload, received = outs[0], got[0][1]
    own = dict(zip(chunks[0], later(plan, place, at, actions, [], chunks[0])[1], strict=True))
    ours = [r for level in chunks[1:] for r in level]
    theirs, more = later(plan, place, at, actions, rest, ours)
    got.append((rest[0], send(theirs[0], CORE)))
    own.update(zip(ours, more, strict=True))

    def terms(lo, hi):
        return [(x, (lo - a) * rows) for (a, b), x in got if a <= lo and hi <= b]

    def total(lo, hi):
        out = own[lo, hi]
        for x, at in terms(lo, hi):
            out = out + x[at : at + out.shape[0]]
        return out

    per = 128 // act
    wide_action = jnp.stack([jnp.pad(w_action, ((j * act, 128 - (j + 1) * act), (0, 0))) for j in range(per)])
    fixed = (act, actions, init_state[None, :], w_state, wide_action, bias[None, :], w_out, reward_vec[None, :])
    done, carry = 0, None
    for i, piece in enumerate(PIECES):
        last = i == len(PIECES) - 1
        piece = steps - done if last else piece * steps // sum(PIECES) // per * per
        carry = rollout(carry, done, piece, steps if last else None, *fixed)
        done += piece
    returns = carry[0]

    for k in range(phases):
        of = (plan.orders[0][k], plan.orders[1][k])
        base = 1 << (phases - 1 - k)
        sent = []
        for i, (lo, hi) in enumerate(chunks[k]):
            if i == 0:
                payload = combine(plan, own[lo, hi], terms(lo, hi), payload, received)
                x = payload
            else:
                x = total(lo, hi)
            x = send(x, of)
            if i == 0:
                received = x
            at = 0 if hi - lo == base else lo - base
            sent.append(((at, at + hi - lo), x))
        got += sent
    pieces = [total(0, 1)]
    for m in bits_of(plan.side):
        pieces += [send(x, (("grp", 2 * m), ("grp", 2 * m))) for x in pieces]
    pieces += [send(x, CORE) for x in pieces]
    new_mean, covariance = finish(plan, place, payload, received, pieces)
    return (new_mean[0], covariance, returns)


def solution(mesh):
    placed = (P(ALL, None), P(ALL), P(), P(), P(), P(), P(), P())
    pops, grps = mesh.shape["pop"], mesh.shape["grp"]

    def run(actions, *rest):
        plan = Plan(pops, grps, actions.shape[1])

        def body(*args):
            return on_device(plan, *args)

        return jax.shard_map(
            body, mesh=mesh, in_specs=placed, out_specs=(P(), P("pop", None), P(ALL)), check_vma=False
        )(actions, *rest)

    return run
```

```python
import functools

import jax
import jax.numpy as jnp
from jax import lax
from jax.experimental import pallas as pl
from jax.experimental.pallas import tpu as pltpu
from jax.sharding import PartitionSpec as P

ALL = ("pop", "grp")
CORE = (("grp", 1), ("grp", 1))
VMEM = pl.BlockSpec(memory_space=pltpu.VMEM)
HBM = pl.BlockSpec(memory_space=pltpu.HBM)
PIECES = (4, 4, 4, 4, 4, 4, 4, 4)


def bits_of(size):
    return [1 << k for k in range(size.bit_length() - 1)]


class Plan:
    def __init__(self, pops, grps, width):
        self.pops, self.grps, self.width = pops, grps, width
        self.side = grps // 2
        self.rows = width // pops
        self.cols = width // grps
        self.tail = (width // self.cols + 1 + 7) // 8 * 8
        pop_dims = [("pop", m) for m in bits_of(pops)]
        grp_dims = [("grp", 2 * m) for m in bits_of(self.side)]
        dims = []
        for k in range(max(len(pop_dims), len(grp_dims))):
            dims += pop_dims[k : k + 1] + grp_dims[k : k + 1]
        other = list(dims)
        for k in range(0, len(dims) - 1, 2):
            other[k], other[k + 1] = dims[k + 1], dims[k]
        self.orders = (dims, other)
        self.phases = len(dims)
        self.blocks = 1 << self.phases
        self.masks = [[self.mask(order, p) for p in range(self.blocks)] for order in self.orders]
        last = max([k for order in self.orders for k, (axis, m) in enumerate(order) if axis == "grp"], default=-1)
        self.run = 1 << (self.phases - 1 - last)
        self.chunks = []
        size = self.blocks
        while size > 1:
            size //= 2
            self.chunks.append([(size + size // 2, 2 * size), (size, size + size // 2)] if size > 1 else [(1, 2)])
        self.chunks.append([(0, 1)])

    def mask(self, order, p):
        pop = grp = 0
        for k, (axis, m) in enumerate(order):
            if p >> (len(order) - 1 - k) & 1:
                pop, grp = (pop ^ m, grp) if axis == "pop" else (pop, grp ^ m)
        return pop * self.side + grp // 2

    def pairs(self, of):
        out = []
        for p in range(self.pops):
            for g in range(self.grps):
                axis, m = of[g & 1]
                q, h = (p ^ m, g) if axis == "pop" else (p, g ^ m)
                out.append((p * self.grps + g, q * self.grps + h))
        return out


def moment_into(plan, other, at_ref, a_ref, ranges, out_refs):
    rows, cols, side, run = plan.rows, plan.cols, plan.side, plan.run
    grp = lax.axis_index("grp")
    here = lax.axis_index("pop") * side + grp // 2
    color = lax.rem(grp + other, 2)
    where = {}
    for (lo, hi), ref in zip(ranges, out_refs, strict=True):
        for p in range(lo, hi):
            where[p] = (ref, (p - lo) * rows)
    for first in range(0, plan.blocks, run):
        if first not in where:
            continue
        places = [here ^ jnp.where(color == 0, plan.masks[0][first + k], plan.masks[1][first + k]) for k in range(run)]
        parts = [at_ref[pl.ds(pl.multiple_of(b // side * rows, rows), rows), :] for b in places]
        lhs = jnp.concatenate(parts, axis=0) if run > 1 else parts[0]
        chunk = color * side + lax.rem(places[0], side)
        rhs = a_ref[:, pl.ds(pl.multiple_of(chunk * cols, cols), cols)]
        got = jnp.dot(lhs, rhs, preferred_element_type=jnp.float32)
        for k in range(run):
            ref, at = where[first + k]
            ref[pl.ds(at, rows), :] = got[k * rows : (k + 1) * rows]


def first_kernel(plan, ranges, cuts, w_hbm, a_hbm, a_ref, at_ref, *refs):
    out_refs, (w_ref, sems) = refs[:-2], refs[-2:]
    height = a_ref.shape[0] // cuts
    copies = [pltpu.make_async_copy(w_hbm, w_ref, sems.at[cuts])]
    for k in range(cuts):
        sl = pl.ds(k * height, height)
        copies.append(pltpu.make_async_copy(a_hbm.at[sl, :], a_ref.at[sl, :], sems.at[k]))
    for copy in copies:
        copy.start()
    copies[0].wait()
    w = w_ref[...].astype(jnp.float32)
    wide = w.astype(jnp.bfloat16)
    for k in range(cuts):
        copies[k + 1].wait()
        sl = pl.ds(k * height, height)
        for c in range(plan.width // 128):
            turned = jnp.transpose(a_ref[sl, c * 128 : (c + 1) * 128])
            at_ref[pl.ds(c * 128, 128), sl] = turned * wide[:, k * height : (k + 1) * height]
    moment_into(plan, 1, at_ref, a_ref, ranges, out_refs)
    tall = jnp.broadcast_to(w, (16, w.shape[1])).astype(jnp.bfloat16)
    sums = jnp.dot(tall, a_ref[...], preferred_element_type=jnp.float32)
    lo, hi = ranges[0]
    base, cols = (hi - lo) * plan.rows, plan.cols
    for k in range(plan.width // cols):
        out_refs[0][pl.ds(base + k, 1), :] = sums[0:1, k * cols : (k + 1) * cols]
    left = plan.tail - plan.width // cols
    total = jnp.sum(w, axis=1, keepdims=True)
    out_refs[0][pl.ds(base + plan.width // cols, left), :] = jnp.broadcast_to(total, (left, cols))


def f32(*shape):
    return jax.ShapeDtypeStruct(shape, jnp.float32)


def first(plan, weight, actions, ranges):
    count, width = actions.shape
    cuts = max(1, min(4, count // 128))
    held = jax.ShapeDtypeStruct((count, width), jnp.bfloat16)
    turned = jax.ShapeDtypeStruct((width, count), jnp.bfloat16)
    outs = [held, turned]
    outs += [f32((hi - lo) * plan.rows + (0 if i else plan.tail), plan.cols) for i, (lo, hi) in enumerate(ranges)]
    return pl.pallas_call(
        functools.partial(first_kernel, plan, ranges, cuts),
        out_shape=outs,
        in_specs=[HBM, HBM],
        out_specs=[VMEM] * len(outs),
        scratch_shapes=[pltpu.VMEM((1, count), jnp.int32), pltpu.SemaphoreType.DMA((cuts + 1,))],
        compiler_params=pltpu.CompilerParams(vmem_limit_bytes=16 << 20),
        cost_estimate=pl.CostEstimate(flops=1 << 29, bytes_accessed=4 << 20, transcendentals=0),
        name="first",
    )(pltpu.with_memory_space_constraint(weight, pltpu.HBM), pltpu.with_memory_space_constraint(actions, pltpu.HBM))


def later_kernel(plan, theirs, ours, at_ref, a_ref, *refs):
    moment_into(plan, 1, at_ref, a_ref, theirs, refs[: len(theirs)])
    moment_into(plan, 0, at_ref, a_ref, ours, refs[len(theirs) :])


def later(plan, at, actions, theirs, ours):
    outs = [f32((hi - lo) * plan.rows, plan.cols) for lo, hi in theirs + ours]
    got = pl.pallas_call(
        functools.partial(later_kernel, plan, theirs, ours),
        out_shape=outs,
        in_specs=[VMEM, VMEM],
        out_specs=[VMEM] * len(outs),
        compiler_params=pltpu.CompilerParams(vmem_limit_bytes=16 << 20),
        cost_estimate=pl.CostEstimate(flops=1 << 29, bytes_accessed=4 << 20, transcendentals=0),
        name="later",
    )(at, actions)
    return got[: len(theirs)], got[len(theirs) :]


def combine_kernel(size, tail, offsets, ends, *refs):
    own_ref, out_ref = refs[0], refs[-1]
    terms, (mine_ref, got_ref) = refs[1:-3], refs[-3:-1]
    out = own_ref[...]
    for ref, at in zip(terms, offsets, strict=True):
        out = out + ref[pl.ds(at, size), :]
    out_ref[pl.ds(0, size), :] = out
    out_ref[pl.ds(size, tail), :] = mine_ref[pl.ds(ends[0], tail), :] + got_ref[pl.ds(ends[1], tail), :]


def combine(plan, own, terms, mine, got):
    size = own.shape[0]
    ends = (mine.shape[0] - plan.tail, got.shape[0] - plan.tail)
    operands = [own] + [x for x, _ in terms] + [mine, got]
    return pl.pallas_call(
        functools.partial(combine_kernel, size, plan.tail, [at for _, at in terms], ends),
        out_shape=f32(size + plan.tail, plan.cols),
        in_specs=[VMEM] * len(operands),
        out_specs=VMEM,
        compiler_params=pltpu.CompilerParams(vmem_limit_bytes=8 << 20),
        cost_estimate=pl.CostEstimate(flops=1 << 18, bytes_accessed=1 << 18, transcendentals=0),
        name="combine",
    )(*operands)


def rollout_kernel(act, first, steps, scale, fresh, a_ref, ws_ref, wa_ref, b_ref, wo_ref, r_ref, *refs):
    per = 128 // act
    if fresh:
        s0_ref, out_refs = refs[0], refs[1:]
        rows = a_ref.shape[0]
        state = jnp.broadcast_to(s0_ref[...], (rows, s0_ref.shape[1]))
        total = jnp.zeros(state.shape, jnp.float32)
    else:
        out_refs = refs[2:]
        state, total = refs[0][...], refs[1][...]
    st_ref, sum_ref = out_refs[-2:]
    st_ref[...] = state
    sum_ref[...] = total

    def body(k, unused):
        off = pl.multiple_of(k * 128, 128)
        for j in range(per):
            st = st_ref[...]
            pre = jnp.dot(st.astype(jnp.bfloat16), ws_ref[...], preferred_element_type=jnp.float32)
            pre = pre + jnp.dot(a_ref[:, pl.ds(off, 128)], wa_ref[j], preferred_element_type=jnp.float32)
            hid = jnp.tanh(pre + b_ref[...]).astype(jnp.bfloat16)
            st = 0.9 * st + jnp.dot(hid, wo_ref[...], preferred_element_type=jnp.float32)
            st_ref[...] = st
            sum_ref[...] += st
        return unused

    lax.fori_loop(first // per, (first + steps) // per, body, 0)
    if scale is not None:
        weighted = sum_ref[...] * r_ref[...]
        ones = jnp.ones((8, weighted.shape[1]), jnp.float32)
        line = lax.dot_general(ones, weighted, (((1,), (1,)), ((), ())), precision=lax.Precision.HIGHEST)
        out_refs[0][...] = line[0:1] / scale


def rollout(carry, first, steps, scale, act, actions, init_state, w_state, wide_action, bias, w_out, reward_vec):
    rows, width = actions.shape[0], init_state.shape[1]
    hidden = w_out.shape[0]
    operands = [actions, w_state, wide_action, bias, w_out, reward_vec]
    operands += [init_state] if carry is None else list(carry)
    last = scale is not None
    flops = 2 * rows * steps * (2 * width * hidden + 128 * hidden)
    return pl.pallas_call(
        functools.partial(rollout_kernel, act, first, steps, scale, carry is None),
        out_shape=f32(1, rows) if last else (f32(rows, width), f32(rows, width)),
        in_specs=[VMEM] * len(operands),
        out_specs=VMEM if last else (VMEM, VMEM),
        scratch_shapes=[pltpu.VMEM((rows, width), jnp.float32)] * (2 if last else 0),
        compiler_params=pltpu.CompilerParams(vmem_limit_bytes=16 << 20),
        cost_estimate=pl.CostEstimate(flops=flops, bytes_accessed=1 << 20, transcendentals=rows * steps * hidden),
        name="rollout",
    )(*operands)


def finish_kernel(plan, ends, mine_ref, got_ref, *refs):
    pieces, (mean_ref, cov_ref, line_ref) = refs[:-3], refs[-3:]
    rows, cols, side = plan.rows, plan.cols, plan.side
    tail = mine_ref[pl.ds(ends[0], plan.tail), :] + got_ref[pl.ds(ends[1], plan.tail), :]
    lines = plan.width // cols
    count = tail[lines : lines + 1]
    inverse = 1.0 / count[:, 0:1]
    for k in range(lines):
        mean_ref[:, pl.ds(k * cols, cols)] = tail[k : k + 1] / count
    pop, grp = lax.axis_index("pop"), lax.axis_index("grp")
    start = pl.multiple_of(pop * rows // 128 * 128, 128)
    column = jnp.transpose(jnp.broadcast_to(mean_ref[:, pl.ds(start, 128)], (128, 128)))
    if rows < 128:
        line_ref[...] = column
        column = line_ref[pl.ds(pl.multiple_of(lax.rem(pop * rows, 128), rows), rows), :]
    left = jnp.concatenate([column] * (cols // 128), axis=1)
    for k, piece in enumerate(pieces):
        color, y = k // side, k % side
        at = (lax.rem(grp, 2) ^ color) * side + ((grp // 2) ^ y)
        sl = pl.ds(pl.multiple_of(at * cols, cols), cols)
        cov_ref[:, sl] = piece[...] * inverse - left * mean_ref[:, sl]


def finish(plan, mine, got, pieces):
    ends = (mine.shape[0] - plan.tail, got.shape[0] - plan.tail)
    return pl.pallas_call(
        functools.partial(finish_kernel, plan, ends),
        out_shape=(f32(1, plan.width), f32(plan.rows, plan.width)),
        in_specs=[VMEM] * (2 + len(pieces)),
        out_specs=(VMEM, VMEM),
        scratch_shapes=[pltpu.VMEM((128, 128), jnp.float32)],
        compiler_params=pltpu.CompilerParams(vmem_limit_bytes=8 << 20),
        name="finish",
    )(mine, got, *pieces)


def on_device(plan, actions, elite_mask, init_state, w_state, w_action, bias, w_out, reward_vec):
    act = w_action.shape[0]
    steps = actions.shape[1] // act
    rows, phases, chunks = plan.rows, plan.phases, plan.chunks

    def send(x, of):
        return lax.ppermute(x, ALL, plan.pairs(of))

    rest = [(0, plan.blocks // 2)]
    actions, at, *outs = first(plan, elite_mask[None, :], actions, chunks[0])
    got = [(r, send(x, CORE)) for r, x in zip(chunks[0], outs, strict=True)]
    payload, received = outs[0], got[0][1]
    own = dict(zip(chunks[0], later(plan, at, actions, [], chunks[0])[1], strict=True))
    ours = [r for level in chunks[1:] for r in level]
    theirs, more = later(plan, at, actions, rest, ours)
    got.append((rest[0], send(theirs[0], CORE)))
    own.update(zip(ours, more, strict=True))

    def terms(lo, hi):
        return [(x, (lo - a) * rows) for (a, b), x in got if a <= lo and hi <= b]

    def total(lo, hi):
        out = own[lo, hi]
        for x, at in terms(lo, hi):
            out = out + x[at : at + out.shape[0]]
        return out

    per = 128 // act
    wide_action = jnp.stack([jnp.pad(w_action, ((j * act, 128 - (j + 1) * act), (0, 0))) for j in range(per)])
    fixed = (act, actions, init_state[None, :], w_state, wide_action, bias[None, :], w_out, reward_vec[None, :])
    done, carry = 0, None
    for i, piece in enumerate(PIECES):
        last = i == len(PIECES) - 1
        piece = steps - done if last else piece * steps // sum(PIECES) // per * per
        carry = rollout(carry, done, piece, steps if last else None, *fixed)
        done += piece
    returns = carry[0]

    for k in range(phases):
        of = (plan.orders[0][k], plan.orders[1][k])
        base = 1 << (phases - 1 - k)
        sent = []
        for i, (lo, hi) in enumerate(chunks[k]):
            if i == 0:
                payload = combine(plan, own[lo, hi], terms(lo, hi), payload, received)
                x = payload
            else:
                x = total(lo, hi)
            x = send(x, of)
            if i == 0:
                received = x
            at = 0 if hi - lo == base else lo - base
            sent.append(((at, at + hi - lo), x))
        got += sent
    pieces = [total(0, 1)]
    for m in bits_of(plan.side):
        pieces += [send(x, (("grp", 2 * m), ("grp", 2 * m))) for x in pieces]
    pieces += [send(x, CORE) for x in pieces]
    new_mean, covariance = finish(plan, payload, received, pieces)
    return (new_mean[0], covariance, returns)


def solution(mesh):
    placed = (P(ALL, None), P(ALL), P(), P(), P(), P(), P(), P())
    pops, grps = mesh.shape["pop"], mesh.shape["grp"]

    def run(actions, *rest):
        plan = Plan(pops, grps, actions.shape[1])

        def body(*args):
            return on_device(plan, *args)

        return jax.shard_map(
            body, mesh=mesh, in_specs=placed, out_specs=(P(), P("pop", None), P(ALL)), check_vma=False
        )(actions, *rest)

    return run
```

```python
import functools

import jax
import jax.numpy as jnp
from jax import lax
from jax.experimental import pallas as pl
from jax.experimental.pallas import tpu as pltpu
from jax.sharding import PartitionSpec as P

ALL = ("pop", "grp")
CORE = (("grp", 1), ("grp", 1))
VMEM = pl.BlockSpec(memory_space=pltpu.VMEM)
HBM = pl.BlockSpec(memory_space=pltpu.HBM)
PIECES = (4, 4, 4, 4, 4, 4, 4, 4)


def bits_of(size):
    return [1 << k for k in range(size.bit_length() - 1)]


class Plan:
    def __init__(self, pops, grps, width):
        self.pops, self.grps, self.width = pops, grps, width
        self.side = grps // 2
        self.rows = width // pops
        self.cols = width // grps
        self.tail = (width // self.cols + 1 + 7) // 8 * 8
        pop_dims = [("pop", m) for m in bits_of(pops)]
        grp_dims = [("grp", 2 * m) for m in bits_of(self.side)]
        dims = []
        for k in range(max(len(pop_dims), len(grp_dims))):
            dims += pop_dims[k : k + 1] + grp_dims[k : k + 1]
        other = list(dims)
        for k in range(0, len(dims) - 1, 2):
            other[k], other[k + 1] = dims[k + 1], dims[k]
        self.orders = (dims, other)
        self.phases = len(dims)
        self.blocks = 1 << self.phases
        self.masks = [[self.mask(order, p) for p in range(self.blocks)] for order in self.orders]
        last = max([k for order in self.orders for k, (axis, m) in enumerate(order) if axis == "grp"], default=-1)
        self.run = 1 << (self.phases - 1 - last)
        self.chunks = []
        size = self.blocks
        while size > 1:
            size //= 2
            half = [list(range(size + size // 2, 2 * size)), list(range(size, size + size // 2))]
            self.chunks.append(half if size > 1 else [[1]])
        self.chunks.append([[0]])

    def mask(self, order, p):
        pop = grp = 0
        for k, (axis, m) in enumerate(order):
            if p >> (len(order) - 1 - k) & 1:
                pop, grp = (pop ^ m, grp) if axis == "pop" else (pop, grp ^ m)
        return pop * self.side + grp // 2

    def pairs(self, of):
        out = []
        for p in range(self.pops):
            for g in range(self.grps):
                axis, m = of[g & 1]
                q, h = (p ^ m, g) if axis == "pop" else (p, g ^ m)
                out.append((p * self.grps + g, q * self.grps + h))
        return out


def moment_into(plan, other, at_ref, a_ref, ranges, out_refs):
    rows, cols, side, run = plan.rows, plan.cols, plan.side, plan.run
    grp = lax.axis_index("grp")
    here = lax.axis_index("pop") * side + grp // 2
    color = lax.rem(grp + other, 2)
    where = {}
    for positions, ref in zip(ranges, out_refs, strict=True):
        for i, p in enumerate(positions):
            where[p] = (ref, i * rows)
    for first in range(0, plan.blocks, run):
        if first not in where:
            continue
        places = [here ^ jnp.where(color == 0, plan.masks[0][first + k], plan.masks[1][first + k]) for k in range(run)]
        parts = [at_ref[pl.ds(pl.multiple_of(b // side * rows, rows), rows), :] for b in places]
        lhs = jnp.concatenate(parts, axis=0) if run > 1 else parts[0]
        chunk = color * side + lax.rem(places[0], side)
        rhs = a_ref[:, pl.ds(pl.multiple_of(chunk * cols, cols), cols)]
        got = jnp.dot(lhs, rhs, preferred_element_type=jnp.float32)
        for k in range(run):
            ref, at = where[first + k]
            ref[pl.ds(at, rows), :] = got[k * rows : (k + 1) * rows]


def first_kernel(plan, ranges, cuts, w_hbm, a_hbm, a_ref, at_ref, *refs):
    out_refs, (w_ref, sems) = refs[:-2], refs[-2:]
    height = a_ref.shape[0] // cuts
    copies = [pltpu.make_async_copy(w_hbm, w_ref, sems.at[cuts])]
    for k in range(cuts):
        sl = pl.ds(k * height, height)
        copies.append(pltpu.make_async_copy(a_hbm.at[sl, :], a_ref.at[sl, :], sems.at[k]))
    for copy in copies:
        copy.start()
    copies[0].wait()
    w = w_ref[...].astype(jnp.float32)
    wide = w.astype(jnp.bfloat16)
    for k in range(cuts):
        copies[k + 1].wait()
        sl = pl.ds(k * height, height)
        for c in range(plan.width // 128):
            turned = jnp.transpose(a_ref[sl, c * 128 : (c + 1) * 128])
            at_ref[pl.ds(c * 128, 128), sl] = turned * wide[:, k * height : (k + 1) * height]
    moment_into(plan, 1, at_ref, a_ref, ranges, out_refs)
    tall = jnp.broadcast_to(w, (16, w.shape[1])).astype(jnp.bfloat16)
    sums = jnp.dot(tall, a_ref[...], preferred_element_type=jnp.float32)
    base, cols = len(ranges[0]) * plan.rows, plan.cols
    for k in range(plan.width // cols):
        out_refs[0][pl.ds(base + k, 1), :] = sums[0:1, k * cols : (k + 1) * cols]
    left = plan.tail - plan.width // cols
    total = jnp.sum(w, axis=1, keepdims=True)
    out_refs[0][pl.ds(base + plan.width // cols, left), :] = jnp.broadcast_to(total, (left, cols))


def f32(*shape):
    return jax.ShapeDtypeStruct(shape, jnp.float32)


def first(plan, weight, actions, ranges):
    count, width = actions.shape
    cuts = max(1, min(4, count // 128))
    held = jax.ShapeDtypeStruct((count, width), jnp.bfloat16)
    turned = jax.ShapeDtypeStruct((width, count), jnp.bfloat16)
    outs = [held, turned]
    outs += [f32(len(r) * plan.rows + (0 if i else plan.tail), plan.cols) for i, r in enumerate(ranges)]
    return pl.pallas_call(
        functools.partial(first_kernel, plan, ranges, cuts),
        out_shape=outs,
        in_specs=[HBM, HBM],
        out_specs=[VMEM] * len(outs),
        scratch_shapes=[pltpu.VMEM((1, count), jnp.int32), pltpu.SemaphoreType.DMA((cuts + 1,))],
        compiler_params=pltpu.CompilerParams(vmem_limit_bytes=16 << 20),
        cost_estimate=pl.CostEstimate(flops=1 << 29, bytes_accessed=4 << 20, transcendentals=0),
        name="first",
    )(pltpu.with_memory_space_constraint(weight, pltpu.HBM), pltpu.with_memory_space_constraint(actions, pltpu.HBM))


def later_kernel(plan, theirs, ours, at_ref, a_ref, *refs):
    moment_into(plan, 1, at_ref, a_ref, theirs, refs[: len(theirs)])
    moment_into(plan, 0, at_ref, a_ref, ours, refs[len(theirs) :])


def later(plan, at, actions, theirs, ours):
    outs = [f32(len(r) * plan.rows, plan.cols) for r in theirs + ours]
    got = pl.pallas_call(
        functools.partial(later_kernel, plan, theirs, ours),
        out_shape=outs,
        in_specs=[VMEM, VMEM],
        out_specs=[VMEM] * len(outs),
        compiler_params=pltpu.CompilerParams(vmem_limit_bytes=16 << 20),
        cost_estimate=pl.CostEstimate(flops=1 << 29, bytes_accessed=4 << 20, transcendentals=0),
        name="later",
    )(at, actions)
    return got[: len(theirs)], got[len(theirs) :]


def combine_kernel(size, tail, offsets, ends, *refs):
    own_ref, out_ref = refs[0], refs[-1]
    terms, (mine_ref, got_ref) = refs[1:-3], refs[-3:-1]
    out = own_ref[...]
    for ref, at in zip(terms, offsets, strict=True):
        out = out + ref[pl.ds(at, size), :]
    out_ref[pl.ds(0, size), :] = out
    out_ref[pl.ds(size, tail), :] = mine_ref[pl.ds(ends[0], tail), :] + got_ref[pl.ds(ends[1], tail), :]


def combine(plan, own, terms, mine, got):
    size = own.shape[0]
    ends = (mine.shape[0] - plan.tail, got.shape[0] - plan.tail)
    operands = [own] + [x for x, _ in terms] + [mine, got]
    return pl.pallas_call(
        functools.partial(combine_kernel, size, plan.tail, [at for _, at in terms], ends),
        out_shape=f32(size + plan.tail, plan.cols),
        in_specs=[VMEM] * len(operands),
        out_specs=VMEM,
        compiler_params=pltpu.CompilerParams(vmem_limit_bytes=8 << 20),
        cost_estimate=pl.CostEstimate(flops=1 << 18, bytes_accessed=1 << 18, transcendentals=0),
        name="combine",
    )(*operands)


def rollout_kernel(act, first, steps, scale, fresh, a_ref, ws_ref, wa_ref, b_ref, wo_ref, r_ref, *refs):
    per = 128 // act
    if fresh:
        s0_ref, out_refs = refs[0], refs[1:]
        rows = a_ref.shape[0]
        state = jnp.broadcast_to(s0_ref[...], (rows, s0_ref.shape[1]))
        total = jnp.zeros(state.shape, jnp.float32)
    else:
        out_refs = refs[2:]
        state, total = refs[0][...], refs[1][...]
    st_ref, sum_ref = out_refs[-2:]
    st_ref[...] = state
    sum_ref[...] = total

    def body(k, unused):
        off = pl.multiple_of(k * 128, 128)
        for j in range(per):
            st = st_ref[...]
            pre = jnp.dot(st.astype(jnp.bfloat16), ws_ref[...], preferred_element_type=jnp.float32)
            pre = pre + jnp.dot(a_ref[:, pl.ds(off, 128)], wa_ref[j], preferred_element_type=jnp.float32)
            hid = jnp.tanh(pre + b_ref[...]).astype(jnp.bfloat16)
            st = 0.9 * st + jnp.dot(hid, wo_ref[...], preferred_element_type=jnp.float32)
            st_ref[...] = st
            sum_ref[...] += st
        return unused

    lax.fori_loop(first // per, (first + steps) // per, body, 0)
    if scale is not None:
        weighted = sum_ref[...] * r_ref[...]
        ones = jnp.ones((8, weighted.shape[1]), jnp.float32)
        line = lax.dot_general(ones, weighted, (((1,), (1,)), ((), ())), precision=lax.Precision.HIGHEST)
        out_refs[0][...] = line[0:1] / scale


def rollout(carry, first, steps, scale, act, actions, init_state, w_state, wide_action, bias, w_out, reward_vec):
    rows, width = actions.shape[0], init_state.shape[1]
    hidden = w_out.shape[0]
    operands = [actions, w_state, wide_action, bias, w_out, reward_vec]
    operands += [init_state] if carry is None else list(carry)
    last = scale is not None
    flops = 2 * rows * steps * (2 * width * hidden + 128 * hidden)
    return pl.pallas_call(
        functools.partial(rollout_kernel, act, first, steps, scale, carry is None),
        out_shape=f32(1, rows) if last else (f32(rows, width), f32(rows, width)),
        in_specs=[VMEM] * len(operands),
        out_specs=VMEM if last else (VMEM, VMEM),
        scratch_shapes=[pltpu.VMEM((rows, width), jnp.float32)] * (2 if last else 0),
        compiler_params=pltpu.CompilerParams(vmem_limit_bytes=16 << 20),
        cost_estimate=pl.CostEstimate(flops=flops, bytes_accessed=1 << 20, transcendentals=rows * steps * hidden),
        name="rollout",
    )(*operands)


def finish_kernel(plan, ends, mine_ref, got_ref, *refs):
    pieces, (mean_ref, cov_ref, line_ref) = refs[:-3], refs[-3:]
    rows, cols, side = plan.rows, plan.cols, plan.side
    tail = mine_ref[pl.ds(ends[0], plan.tail), :] + got_ref[pl.ds(ends[1], plan.tail), :]
    lines = plan.width // cols
    count = tail[lines : lines + 1]
    inverse = 1.0 / count[:, 0:1]
    for k in range(lines):
        mean_ref[:, pl.ds(k * cols, cols)] = tail[k : k + 1] / count
    pop, grp = lax.axis_index("pop"), lax.axis_index("grp")
    start = pl.multiple_of(pop * rows // 128 * 128, 128)
    column = jnp.transpose(jnp.broadcast_to(mean_ref[:, pl.ds(start, 128)], (128, 128)))
    if rows < 128:
        line_ref[...] = column
        column = line_ref[pl.ds(pl.multiple_of(lax.rem(pop * rows, 128), rows), rows), :]
    left = jnp.concatenate([column] * (cols // 128), axis=1)
    for k, piece in enumerate(pieces):
        color, y = k // side, k % side
        at = (lax.rem(grp, 2) ^ color) * side + ((grp // 2) ^ y)
        sl = pl.ds(pl.multiple_of(at * cols, cols), cols)
        cov_ref[:, sl] = piece[...] * inverse - left * mean_ref[:, sl]


def finish(plan, mine, got, pieces):
    ends = (mine.shape[0] - plan.tail, got.shape[0] - plan.tail)
    return pl.pallas_call(
        functools.partial(finish_kernel, plan, ends),
        out_shape=(f32(1, plan.width), f32(plan.rows, plan.width)),
        in_specs=[VMEM] * (2 + len(pieces)),
        out_specs=(VMEM, VMEM),
        scratch_shapes=[pltpu.VMEM((128, 128), jnp.float32)],
        compiler_params=pltpu.CompilerParams(vmem_limit_bytes=8 << 20),
        name="finish",
    )(mine, got, *pieces)


def on_device(plan, actions, elite_mask, init_state, w_state, w_action, bias, w_out, reward_vec):
    act = w_action.shape[0]
    steps = actions.shape[1] // act
    rows, phases, chunks = plan.rows, plan.phases, plan.chunks

    def send(x, of):
        return lax.ppermute(x, ALL, plan.pairs(of))

    rest = list(range(plan.blocks // 2))
    actions, at, *outs = first(plan, elite_mask[None, :], actions, chunks[0])
    got = [(r, send(x, CORE)) for r, x in zip(chunks[0], outs, strict=True)]
    payload, received = outs[0], got[0][1]
    mine = later(plan, at, actions, [], chunks[0])[1]
    ours = [r for level in chunks[1:] for r in level]
    theirs, more = later(plan, at, actions, [rest], ours)
    got.append((rest, send(theirs[0], CORE)))
    own = {tuple(r): x for r, x in zip(chunks[0] + ours, list(mine) + list(more), strict=True)}

    def terms(positions):
        out = []
        for held, x in got:
            if set(positions) <= set(held):
                at = held.index(positions[0])
                assert held[at : at + len(positions)] == positions
                out.append((x, at * rows))
        return out

    def total(positions):
        out = own[tuple(positions)]
        for x, at in terms(positions):
            out = out + x[at : at + out.shape[0]]
        return out

    per = 128 // act
    wide_action = jnp.stack([jnp.pad(w_action, ((j * act, 128 - (j + 1) * act), (0, 0))) for j in range(per)])
    fixed = (act, actions, init_state[None, :], w_state, wide_action, bias[None, :], w_out, reward_vec[None, :])
    done, carry = 0, None
    for i, piece in enumerate(PIECES):
        last = i == len(PIECES) - 1
        piece = steps - done if last else piece * steps // sum(PIECES) // per * per
        carry = rollout(carry, done, piece, steps if last else None, *fixed)
        done += piece
    returns = carry[0]

    for k in range(phases):
        of = (plan.orders[0][k], plan.orders[1][k])
        base = 1 << (phases - 1 - k)
        sent = []
        for i, positions in enumerate(chunks[k]):
            if i == 0:
                payload = combine(plan, own[tuple(positions)], terms(positions), payload, received)
                received = x = send(payload, of)
            else:
                x = send(total(positions), of)
            sent.append(([p - base for p in positions], x))
        got += sent
    pieces = [total([0])]
    for m in bits_of(plan.side):
        pieces += [send(x, (("grp", 2 * m), ("grp", 2 * m))) for x in pieces]
    pieces += [send(x, CORE) for x in pieces]
    new_mean, covariance = finish(plan, payload, received, pieces)
    return (new_mean[0], covariance, returns)


def solution(mesh):
    placed = (P(ALL, None), P(ALL), P(), P(), P(), P(), P(), P())
    pops, grps = mesh.shape["pop"], mesh.shape["grp"]

    def run(actions, *rest):
        plan = Plan(pops, grps, actions.shape[1])

        def body(*args):
            return on_device(plan, *args)

        return jax.shard_map(
            body, mesh=mesh, in_specs=placed, out_specs=(P(), P("pop", None), P(ALL)), check_vma=False
        )(actions, *rest)

    return run
```
